32 devices in a mesh: grp: 4 (over y, x), word: 8 (over z, core).
Axes of the slice: x: 2, y: 2, z: 4, core: 2. Of those that a mesh axis runs over, the one named last changes fastest.
Arguments:
- descriptors: bfloat16 [262144, 128], P(('grp', 'word'))
- word_ids: int32 [262144], P(('grp', 'word')), may hold values from 0 to 1023, as said below
Outputs:
- centroids: bfloat16 [1024, 128], P('word')
- nearest: float32 [262144], P(('grp', 'word'))
The draws below stay inside these ranges and needn't reach their ends.
Inputs may be any that keep to these rules, and one draw needn't show every extreme that they name: `word_ids`: the word ids of one device's descriptors lie in a window of 64 consecutive ids, counted modulo 1024; every word id from 0 to 1023 occurs at least once.
All inputs are finite; a program needn't handle non-finite values.
Results may differ from the reference program's by a relative error of at most 0.0015.
Values may be sent and summed in bfloat16 or wider, within the bound.
No kernel may reach another device: no remote copies, remote signals or barrier semaphores. Data moves between devices by JAX's collectives and lax.ppermute only.
A program may use at most 64 MiB of HBM per device.

```python
import jax
import jax.numpy as jnp
from jax import lax

D = 128
K = 1024
SPREAD = 64
ROWS_DEV = 8192
ROWS = 262144


def make_ids(key):
    blocks = ROWS // ROWS_DEV
    half = min(ROWS_DEV, SPREAD // 2)
    order = jax.random.permutation(jax.random.fold_in(key, 13), blocks).astype(jnp.int32)
    anchor = order % (K // half) * half
    lag = jax.random.randint(jax.random.fold_in(key, 11), (blocks,), 0, SPREAD - half + 1)
    start = (anchor - lag) % K
    jitter = jax.random.randint(jax.random.fold_in(key, 12), (blocks, ROWS_DEV), 0, SPREAD)
    window_ids = (start[:, None] + jitter) % K
    shift = jax.random.randint(jax.random.fold_in(key, 14), (blocks,), 0, ROWS_DEV)
    column = jnp.arange(ROWS_DEV, dtype=jnp.int32)
    place = (column[None, :] + shift[:, None]) % ROWS_DEV
    cover_ids = (anchor[:, None] + place) % K
    ids = jnp.where(place < half, cover_ids, window_ids)
    return ids.reshape(ROWS).astype(jnp.int32)


def draw_word_ids(key, part):
    return make_ids(key)


def draw_descriptors(key, part):
    ids = make_ids(key)
    stale = jax.random.randint(jax.random.fold_in(key, 24), (ROWS,), 0, 20) < 7
    other = jax.random.randint(jax.random.fold_in(key, 25), (ROWS,), 0, K)
    source = jnp.where(stale, other, ids)
    centers = jax.random.normal(jax.random.fold_in(key, 21), (K, D), jnp.float32)
    direction = jax.random.normal(jax.random.fold_in(key, 22), (D,), jnp.float32)
    position = jnp.arange(ROWS, dtype=jnp.float32) / ROWS
    noise = jax.random.normal(jax.random.fold_in(key, 23), (ROWS, D), jnp.float32)
    values = jnp.take(centers, source, axis=0) + 1.5 * (2.0 * position - 1.0)[:, None] * direction[None, :] + noise
    return values.astype(jnp.bfloat16)


def setup_inputs(seed: int = 0) -> dict:
    seeds = jax.random.split(jax.random.key(seed), 3)
    descriptors = draw_descriptors(jax.random.fold_in(seeds[2], 71), 0)
    word_ids = draw_word_ids(jax.random.fold_in(seeds[2], 71), 0)
    return {"descriptors": descriptors, "word_ids": word_ids}


def reference(descriptors, word_ids):
    ids = word_ids.astype(jnp.int32)
    sums = jax.ops.segment_sum(descriptors.astype(jnp.float32), ids, num_segments=K)
    counts = jax.ops.segment_sum(jnp.ones(ids.shape, jnp.float32), ids, num_segments=K)
    cent = (sums / counts[:, None]).astype(jnp.bfloat16)
    cf = cent.astype(jnp.float32)
    cnorm = jnp.sum(cf * cf, axis=1)
    block = min(4096, ROWS)
    xs = descriptors.reshape(ROWS // block, block, D)

    def one(xb):
        xf = xb.astype(jnp.float32)
        xnorm = jnp.sum(xf * xf, axis=1)
        dots = jnp.dot(xb, cent.T, preferred_element_type=jnp.float32)
        dist = (xnorm[:, None] - 2.0 * dots + cnorm[None, :]) / D
        return jnp.min(dist, axis=1)

    nearest = lax.map(one, xs).reshape(ROWS)
    return cent, nearest
```

```python
import functools

import jax
import jax.numpy as jnp
from jax import lax
from jax.experimental import pallas as pl
from jax.experimental.pallas import tpu as pltpu
from jax.sharding import PartitionSpec as P

K = 1024
SPREAD = 64
HALF = SPREAD // 2
AUX = 8
BOTH = ("grp", "word")
F32 = jnp.float32
BF16 = jnp.bfloat16
NT = (((1,), (1,)), ((), ()))
VMEM = pl.BlockSpec(memory_space=pltpu.VMEM)
HBM = pl.BlockSpec(memory_space=pltpu.HBM)
SMALL = pltpu.CompilerParams(vmem_limit_bytes=16 << 20)


def split3(v):
    hi = v.astype(BF16)
    rest = v - hi.astype(F32)
    mid = rest.astype(BF16)
    low = (rest - mid.astype(F32)).astype(BF16)
    return hi, mid, low


def sums_kernel(ids_hbm, x_hbm, keep_ref, send_ref, ids_ref, x_ref, sem):
    core = lax.axis_index("word") % 2
    load_ids = pltpu.make_async_copy(ids_hbm, ids_ref, sem.at[0])
    load_ids.start()
    load = pltpu.make_async_copy(x_hbm, x_ref, sem.at[1])
    load.start()
    load_ids.wait()
    slot = lax.broadcasted_iota(jnp.int32, (SPREAD, 128), 0)
    ids = ids_ref[...]
    at = jnp.bitwise_and(ids, SPREAD - 1)
    total = jnp.zeros((SPREAD, 128), F32)
    pieces = []
    for r in range(ids.shape[0]):
        hit = jnp.where(slot == at[r : r + 1, :], 1.0, 0.0)
        total = total + hit
        pieces.append(hit.astype(BF16))
    first = ids[0:1, 0:1]
    rel = jnp.bitwise_and(ids - first + K // 2, K - 1)
    low = jnp.min(jnp.min(rel, axis=0, keepdims=True), axis=1, keepdims=True)
    start = jnp.bitwise_and(first + low - K // 2, K - 1)
    lane = lax.broadcasted_iota(jnp.int32, (AUX, 128), 1)
    own = jnp.bitwise_and(lane, SPREAD - 1)
    word = jnp.bitwise_and(start + jnp.bitwise_and(own - start, SPREAD - 1), K - 1)
    place = ((word // SPREAD) * HALF + jnp.bitwise_and(word, HALF - 1)).astype(F32)
    column = jnp.sum(total, axis=1, keepdims=True)
    wide = jnp.broadcast_to(column, (SPREAD, 128))
    row = jnp.concatenate([wide, wide], axis=0).T[0:AUX, :]
    aux0 = jnp.where(lane < HALF, place, pltpu.roll(row, HALF, 1))
    aux1 = jnp.where(lane < HALF, pltpu.roll(place, 128 - HALF, 1), row)
    aux0 = jnp.where(lane < SPREAD, aux0, 0.0)
    aux1 = jnp.where(lane < SPREAD, aux1, 0.0)
    keep_ref[HALF : HALF + AUX, :] = jnp.where(core == 0, aux0, aux1)
    send_ref[HALF : HALF + AUX, :] = pltpu.roll(jnp.where(core == 0, aux1, aux0), SPREAD, 1)
    load.wait()
    sums = jnp.dot(jnp.concatenate(pieces, axis=1), x_ref[...], preferred_element_type=F32)
    keep_ref[0:HALF, :] = jnp.where(core == 0, sums[0:HALF], sums[HALF:SPREAD])
    send_ref[0:HALF, :] = jnp.where(core == 0, sums[HALF:SPREAD], sums[0:HALF])


def window_sums(ids, x):
    rows, depth = x.shape
    out = jax.ShapeDtypeStruct((HALF + AUX, depth), F32)
    return pl.pallas_call(
        sums_kernel,
        in_specs=[HBM, HBM],
        out_specs=(VMEM, VMEM),
        out_shape=(out, out),
        scratch_shapes=[
            pltpu.VMEM((rows // 128, 128), jnp.int32),
            pltpu.VMEM((rows, depth), BF16),
            pltpu.SemaphoreType.DMA((2,)),
        ],
        compiler_params=SMALL,
        name="window_sums",
    )(pltpu.with_memory_space_constraint(ids, pltpu.HBM), pltpu.with_memory_space_constraint(x, pltpu.HBM))


def norms_kernel(x_ref, out_ref):
    n = x_ref.shape[0]
    xf = x_ref[...].astype(F32)
    sq = xf * xf
    hi = sq.astype(BF16)
    low = (sq - hi.astype(F32)).astype(BF16)
    both = jnp.concatenate([hi, low], axis=1)
    ones = jnp.ones((8, both.shape[1]), BF16)
    row = lax.dot_general(ones, both, NT, preferred_element_type=F32)
    for r in range(n // 128):
        out_ref[r : r + 1, :] = row[0:1, r * 128 : (r + 1) * 128]


def norms(x):
    rows, depth = x.shape
    chunk = min(2048, rows)
    return pl.pallas_call(
        norms_kernel,
        grid=(rows // chunk,),
        in_specs=[pl.BlockSpec((chunk, depth), lambda i: (i, 0))],
        out_specs=pl.BlockSpec((chunk // 128, 128), lambda i: (i, 0)),
        out_shape=jax.ShapeDtypeStruct((rows // 128, 128), F32),
        cost_estimate=pl.CostEstimate(flops=2 * rows * depth, bytes_accessed=2 * rows * depth, transcendentals=0),
        compiler_params=SMALL,
        name="norms",
    )(x)


def means_kernel(parts, *refs):
    ins, out_ref = refs[:parts], refs[parts]
    rows = ins[0].shape[0] - AUX
    half = out_ref.shape[0]
    target = lax.broadcasted_iota(jnp.int32, (half, 128), 0).astype(F32)
    pieces, values = [], []
    count = jnp.zeros((half, 128), F32)
    for ref in ins:
        for pair in range(rows // 128):
            a = ref[rows + 2 * pair : rows + 2 * pair + 1, :]
            b = ref[rows + 2 * pair + 1 : rows + 2 * pair + 2, :]
            lane = lax.broadcasted_iota(jnp.int32, (1, 128), 1)
            pa = jnp.where(lane < 32, a, pltpu.roll(a, 96, 1))
            ca = jnp.where(lane < 32, pltpu.roll(a, 96, 1), pltpu.roll(a, 64, 1))
            pb = jnp.where(lane < 96, pltpu.roll(b, 64, 1), pltpu.roll(b, 32, 1))
            cb = jnp.where(lane < 96, pltpu.roll(b, 32, 1), b)
            place = jnp.where(lane < 64, pa, pb)
            amount = jnp.where(lane < 64, ca, cb)
            hit = target == place
            count = count + jnp.where(hit, amount, 0.0)
            pieces.append(jnp.where(hit, 1.0, 0.0).astype(BF16))
            values.append(jnp.concatenate(split3(ref[128 * pair : 128 * pair + 128, :]), axis=1))
    onehot = jnp.concatenate(pieces, axis=1)
    table = jnp.concatenate(values, axis=0)
    wide = jnp.dot(onehot, table, preferred_element_type=F32)
    sums = wide[:, 0:128] + wide[:, 128:256] + wide[:, 256:384]
    out_ref[...] = (sums / jnp.sum(count, axis=1, keepdims=True)).astype(BF16)


def means(parts, half):
    depth = parts[0].shape[1]
    return pl.pallas_call(
        functools.partial(means_kernel, len(parts)),
        in_specs=[VMEM] * len(parts),
        out_specs=VMEM,
        compiler_params=SMALL,
        out_shape=jax.ShapeDtypeStruct((half, depth), BF16),
        name="means",
    )(*parts)


def nearest_kernel(last, cent_ref, x_ref, *refs):
    if last:
        near_ref, norm_ref, out_ref, table = refs
    else:
        out_ref, table = refs
    words, depth = cent_ref.shape
    n = x_ref.shape[0]

    cf = cent_ref[...].astype(F32)
    norm = jnp.broadcast_to(0.5 * jnp.sum(cf * cf, axis=1, keepdims=True), (words, depth))
    lane = lax.broadcasted_iota(jnp.int32, (words, depth), 1)
    hi, mid, low = [p.astype(F32) for p in split3(norm)]
    extra = jnp.where(lane == 0, hi, jnp.where(lane == 1, mid, jnp.where(lane == 2, low, 0.0)))
    table[:, 0:depth] = (-2.0 * cf).astype(BF16)
    table[:, depth : 2 * depth] = extra.astype(BF16)
    cols = 256
    twos = jnp.full((cols, depth), 2.0, BF16)
    for t in range(n // cols):
        full = jnp.concatenate([x_ref[t * cols : (t + 1) * cols, :], twos], axis=1)
        d = lax.dot_general(table[...], full, NT, preferred_element_type=F32)
        row = jnp.min(jnp.min(d.reshape(words // 8, 8, cols), axis=0), axis=0, keepdims=True)
        for r in range(cols // 128):
            at = t * (cols // 128) + r
            value = row[0:1, r * 128 : (r + 1) * 128]
            if last:
                value = jnp.minimum(value, near_ref[at : at + 1, :])
                value = (value + norm_ref[at : at + 1, :]) * (1.0 / depth)
            out_ref[at : at + 1, :] = value


def nearest(cent, x, near=None, norm=None):
    rows, depth = x.shape
    words = cent.shape[0]
    last = near is not None
    return pl.pallas_call(
        functools.partial(nearest_kernel, last),
        in_specs=[VMEM] * (4 if last else 2),
        out_specs=VMEM,
        out_shape=jax.ShapeDtypeStruct((rows // 128, 128), F32),
        scratch_shapes=[pltpu.VMEM((words, 2 * depth), BF16)],
        cost_estimate=pl.CostEstimate(flops=4 * rows * depth * words, bytes_accessed=2 * rows * depth, transcendentals=0),
        compiler_params=SMALL,
        name="nearest_last" if last else "nearest_first",
    )(*((cent, x, near, norm) if last else (cent, x)))


def moved(a, axis, size, flip):
    return lax.ppermute(a, axis, [(i, i ^ flip) for i in range(size)])


def gathered(groups, words, descriptors, word_ids):
    rows, depth = descriptors.shape
    ids = word_ids.reshape(rows // 128, 128)
    keep, send = window_sums(ids, descriptors)
    got = moved(send, "word", words, 1)
    mine = jnp.concatenate([keep[:HALF], got[:HALF], keep[HALF:] + got[HALF:]], axis=0)
    line = [mine] + [moved(mine, "word", words, 2 * k) for k in range(1, words // 2)]
    aux = [a[SPREAD : SPREAD + 1] for a in line]
    aux.append(jnp.zeros((-len(line) % AUX, depth), F32))
    block = jnp.concatenate([a[:SPREAD] for a in line] + aux, axis=0)
    blocks = [block] + [moved(block, "grp", groups, k) for k in range(1, groups)]
    xnorm = norms(descriptors)
    half = means(blocks, K // 2)
    other = moved(half, "word", words, 1)
    near = nearest(half, descriptors)
    near = nearest(other, descriptors, near, xnorm)
    index = lax.axis_index("word")
    owned = K // words
    cut = [lax.dynamic_slice_in_dim(h, index * (owned // 2), owned // 2, 0) for h in (half, other)]
    cut = [c.reshape(owned // SPREAD, 1, HALF, depth) for c in cut]
    even = index % 2 == 0
    cent = jnp.concatenate([jnp.where(even, cut[0], cut[1]), jnp.where(even, cut[1], cut[0])], axis=1)
    return cent.reshape(owned, depth), near.reshape(rows)


def summed(words, descriptors, word_ids):
    rows, depth = descriptors.shape
    keep, send = window_sums(word_ids.reshape(rows // 128, 128), descriptors)
    index = lax.axis_index("word")
    even = index % 2 == 0
    near_half = jnp.where(even, keep, send)
    far_half = jnp.where(even, send, keep)
    target = lax.broadcasted_iota(jnp.int32, (K // 2, HALF), 0)
    totals, counts = [], []
    for part in (near_half, far_half):
        aux = part[HALF, :SPREAD] + part[HALF, SPREAD:]
        hit = target == aux[None, :HALF].astype(jnp.int32)
        counts.append(jnp.sum(jnp.where(hit, aux[None, HALF:], 0.0), axis=1))
        totals.append(jnp.dot(hit.astype(F32), part[:HALF], precision=lax.Precision.HIGHEST))
    total, count = lax.psum((jnp.concatenate(totals), jnp.concatenate(counts)), BOTH)
    cent = (total / count[:, None]).astype(BF16)
    near = nearest(cent[: K // 2], descriptors)
    near = nearest(cent[K // 2 :], descriptors, near, norms(descriptors))
    cent = cent.reshape(2, K // SPREAD, HALF, depth).swapaxes(0, 1).reshape(K, depth)
    owned = K // words
    return lax.dynamic_slice_in_dim(cent, index * owned, owned, 0), near.reshape(rows)


def solution(mesh):
    groups, words = mesh.shape["grp"], mesh.shape["word"]
    small = groups * words * SPREAD <= 2 * K and K // words >= SPREAD
    return jax.shard_map(
        functools.partial(gathered, groups, words) if small else functools.partial(summed, words),
        mesh=mesh,
        in_specs=(P(BOTH, None), P(BOTH)),
        out_specs=(P("word", None), P(BOTH)),
        check_vma=False,
    )
```

```python
import functools

import jax
import jax.numpy as jnp
from jax import lax
from jax.experimental import pallas as pl
from jax.experimental.pallas import tpu as pltpu
from jax.sharding import PartitionSpec as P

K = 1024
SPREAD = 64
HALF = SPREAD // 2
AUX = 8
BOTH = ("grp", "word")
F32 = jnp.float32
BF16 = jnp.bfloat16
NT = (((1,), (1,)), ((), ()))
VMEM = pl.BlockSpec(memory_space=pltpu.VMEM)
HBM = pl.BlockSpec(memory_space=pltpu.HBM)
SMALL = pltpu.CompilerParams(vmem_limit_bytes=16 << 20)


def split3(v):
    hi = v.astype(BF16)
    rest = v - hi.astype(F32)
    mid = rest.astype(BF16)
    low = (rest - mid.astype(F32)).astype(BF16)
    return hi, mid, low


def sums_kernel(ids_hbm, x_hbm, keep_ref, send_ref, x_ref, ids_ref, sem):
    core = lax.axis_index("word") % 2
    load_ids = pltpu.make_async_copy(ids_hbm, ids_ref, sem.at[0])
    load_ids.start()
    load = pltpu.make_async_copy(x_hbm, x_ref, sem.at[1])
    load.start()
    load_ids.wait()
    slot = lax.broadcasted_iota(jnp.int32, (SPREAD, 128), 0)
    ids = ids_ref[...]
    at = jnp.bitwise_and(ids, SPREAD - 1)
    total = jnp.zeros((SPREAD, 128), F32)
    pieces = []
    for r in range(ids.shape[0]):
        hit = jnp.where(slot == at[r : r + 1, :], 1.0, 0.0)
        total = total + hit
        pieces.append(hit.astype(BF16))
    first = ids[0:1, 0:1]
    rel = jnp.bitwise_and(ids - first + K // 2, K - 1)
    low = jnp.min(jnp.min(rel, axis=0, keepdims=True), axis=1, keepdims=True)
    start = jnp.bitwise_and(first + low - K // 2, K - 1)
    lane = lax.broadcasted_iota(jnp.int32, (AUX, 128), 1)
    own = jnp.bitwise_and(lane, SPREAD - 1)
    word = jnp.bitwise_and(start + jnp.bitwise_and(own - start, SPREAD - 1), K - 1)
    place = ((word // SPREAD) * HALF + jnp.bitwise_and(word, HALF - 1)).astype(F32)
    column = jnp.sum(total, axis=1, keepdims=True)
    wide = jnp.broadcast_to(column, (SPREAD, 128))
    row = jnp.concatenate([wide, wide], axis=0).T[0:AUX, :]
    aux0 = jnp.where(lane < HALF, place, pltpu.roll(row, HALF, 1))
    aux1 = jnp.where(lane < HALF, pltpu.roll(place, 128 - HALF, 1), row)
    aux0 = jnp.where(lane < SPREAD, aux0, 0.0)
    aux1 = jnp.where(lane < SPREAD, aux1, 0.0)
    keep_ref[HALF : HALF + AUX, :] = jnp.where(core == 0, aux0, aux1)
    send_ref[HALF : HALF + AUX, :] = pltpu.roll(jnp.where(core == 0, aux1, aux0), SPREAD, 1)
    load.wait()
    sums = jnp.dot(jnp.concatenate(pieces, axis=1), x_ref[...], preferred_element_type=F32)
    keep_ref[0:HALF, :] = jnp.where(core == 0, sums[0:HALF], sums[HALF:SPREAD])
    send_ref[0:HALF, :] = jnp.where(core == 0, sums[HALF:SPREAD], sums[0:HALF])


def window_sums(ids, x):
    rows, depth = x.shape
    out = jax.ShapeDtypeStruct((HALF + AUX, depth), F32)
    return pl.pallas_call(
        sums_kernel,
        in_specs=[HBM, HBM],
        out_specs=(VMEM, VMEM, VMEM),
        out_shape=(out, out, jax.ShapeDtypeStruct(x.shape, x.dtype)),
        scratch_shapes=[pltpu.VMEM((rows // 128, 128), jnp.int32), pltpu.SemaphoreType.DMA((2,))],
        compiler_params=SMALL,
        name="window_sums",
    )(pltpu.with_memory_space_constraint(ids, pltpu.HBM), pltpu.with_memory_space_constraint(x, pltpu.HBM))


def norms_kernel(x_ref, out_ref):
    n = x_ref.shape[0]
    xf = x_ref[...].astype(F32)
    sq = xf * xf
    hi = sq.astype(BF16)
    low = (sq - hi.astype(F32)).astype(BF16)
    both = jnp.concatenate([hi, low], axis=1)
    ones = jnp.ones((8, both.shape[1]), BF16)
    row = lax.dot_general(ones, both, NT, preferred_element_type=F32)
    for r in range(n // 128):
        out_ref[r : r + 1, :] = row[0:1, r * 128 : (r + 1) * 128]


def norms(x):
    rows, depth = x.shape
    chunk = min(2048, rows)
    return pl.pallas_call(
        norms_kernel,
        grid=(rows // chunk,),
        in_specs=[pl.BlockSpec((chunk, depth), lambda i: (i, 0))],
        out_specs=pl.BlockSpec((chunk // 128, 128), lambda i: (i, 0)),
        out_shape=jax.ShapeDtypeStruct((rows // 128, 128), F32),
        cost_estimate=pl.CostEstimate(flops=2 * rows * depth, bytes_accessed=2 * rows * depth, transcendentals=0),
        compiler_params=SMALL,
        name="norms",
    )(x)


def means_kernel(parts, *refs):
    ins, out_ref = refs[:parts], refs[parts]
    rows = ins[0].shape[0] - AUX
    half = out_ref.shape[0]
    target = lax.broadcasted_iota(jnp.int32, (half, 128), 0).astype(F32)
    pieces, values = [], []
    count = jnp.zeros((half, 128), F32)
    for ref in ins:
        for pair in range(rows // 128):
            a = ref[rows + 2 * pair : rows + 2 * pair + 1, :]
            b = ref[rows + 2 * pair + 1 : rows + 2 * pair + 2, :]
            lane = lax.broadcasted_iota(jnp.int32, (1, 128), 1)
            pa = jnp.where(lane < 32, a, pltpu.roll(a, 96, 1))
            ca = jnp.where(lane < 32, pltpu.roll(a, 96, 1), pltpu.roll(a, 64, 1))
            pb = jnp.where(lane < 96, pltpu.roll(b, 64, 1), pltpu.roll(b, 32, 1))
            cb = jnp.where(lane < 96, pltpu.roll(b, 32, 1), b)
            place = jnp.where(lane < 64, pa, pb)
            amount = jnp.where(lane < 64, ca, cb)
            hit = target == place
            count = count + jnp.where(hit, amount, 0.0)
            pieces.append(jnp.where(hit, 1.0, 0.0).astype(BF16))
            values.append(jnp.concatenate(split3(ref[128 * pair : 128 * pair + 128, :]), axis=1))
    onehot = jnp.concatenate(pieces, axis=1)
    table = jnp.concatenate(values, axis=0)
    wide = jnp.dot(onehot, table, preferred_element_type=F32)
    sums = wide[:, 0:128] + wide[:, 128:256] + wide[:, 256:384]
    out_ref[...] = (sums / jnp.sum(count, axis=1, keepdims=True)).astype(BF16)


def means(parts, half):
    depth = parts[0].shape[1]
    return pl.pallas_call(
        functools.partial(means_kernel, len(parts)),
        in_specs=[VMEM] * len(parts),
        out_specs=VMEM,
        compiler_params=SMALL,
        out_shape=jax.ShapeDtypeStruct((half, depth), BF16),
        name="means",
    )(*parts)


def own_words(mine_ref, other_ref, own_ref):
    index = lax.axis_index("word")
    even = index % 2 == 0
    blocks = own_ref.shape[0] // SPREAD
    for b in range(blocks):
        rows = pl.ds(pl.multiple_of((index * blocks + b) * HALF, HALF), HALF)
        mine, other = mine_ref[rows, :], other_ref[rows, :]
        own_ref[b * SPREAD : b * SPREAD + HALF, :] = jnp.where(even, mine, other)
        own_ref[b * SPREAD + HALF : (b + 1) * SPREAD, :] = jnp.where(even, other, mine)


def nearest_kernel(last, cent_ref, x_ref, *refs):
    if last:
        mine_ref, near_ref, norm_ref, own_ref, out_ref, table = refs
        own_words(mine_ref, cent_ref, own_ref)
    else:
        out_ref, table = refs
    words, depth = cent_ref.shape
    n = x_ref.shape[0]

    cf = cent_ref[...].astype(F32)
    norm = jnp.broadcast_to(0.5 * jnp.sum(cf * cf, axis=1, keepdims=True), (words, depth))
    lane = lax.broadcasted_iota(jnp.int32, (words, depth), 1)
    hi, mid, low = [p.astype(F32) for p in split3(norm)]
    extra = jnp.where(lane == 0, hi, jnp.where(lane == 1, mid, jnp.where(lane == 2, low, 0.0)))
    table[:, 0:depth] = (-2.0 * cf).astype(BF16)
    table[:, depth : 2 * depth] = extra.astype(BF16)
    cols = 256
    twos = jnp.full((cols, depth), 2.0, BF16)
    for t in range(n // cols):
        full = jnp.concatenate([x_ref[t * cols : (t + 1) * cols, :], twos], axis=1)
        d = lax.dot_general(table[...], full, NT, preferred_element_type=F32)
        row = jnp.min(jnp.min(d.reshape(words // 8, 8, cols), axis=0), axis=0, keepdims=True)
        for r in range(cols // 128):
            at = t * (cols // 128) + r
            value = row[0:1, r * 128 : (r + 1) * 128]
            if last:
                value = jnp.minimum(value, near_ref[at : at + 1, :])
                value = (value + norm_ref[at : at + 1, :]) * (1.0 / depth)
            out_ref[at : at + 1, :] = value


def nearest(cent, x, *last, owned=0):
    rows, depth = x.shape
    words = cent.shape[0]
    out = jax.ShapeDtypeStruct((rows // 128, 128), F32)
    own = jax.ShapeDtypeStruct((owned, depth), BF16)
    return pl.pallas_call(
        functools.partial(nearest_kernel, bool(last)),
        in_specs=[VMEM] * (2 + len(last)),
        out_specs=(VMEM, VMEM) if last else VMEM,
        out_shape=(own, out) if last else out,
        scratch_shapes=[pltpu.VMEM((words, 2 * depth), BF16)],
        cost_estimate=pl.CostEstimate(flops=4 * rows * depth * words, bytes_accessed=2 * rows * depth, transcendentals=0),
        compiler_params=SMALL,
        name="nearest_last" if last else "nearest_first",
    )(cent, x, *last)


def moved(a, axis, size, flip):
    return lax.ppermute(a, axis, [(i, i ^ flip) for i in range(size)])


def far_first(size):
    return list(range(size // 2, size)) + list(range(1, size // 2))


def gathered(groups, words, descriptors, word_ids):
    rows, depth = descriptors.shape
    ids = word_ids.reshape(rows // 128, 128)
    keep, send, x = window_sums(ids, descriptors)
    got = moved(send, "word", words, 1)
    mine = jnp.concatenate([keep[:HALF], got[:HALF], keep[HALF:] + got[HALF:]], axis=0)
    line = [mine] + [moved(mine, "word", words, 2 * k) for k in far_first(words // 2)]
    aux = [a[SPREAD : SPREAD + 1] for a in line]
    aux.append(jnp.zeros((-len(line) % AUX, depth), F32))
    block = jnp.concatenate([a[:SPREAD] for a in line] + aux, axis=0)
    blocks = [block] + [moved(block, "grp", groups, k) for k in range(groups - 1, 0, -1)]
    xnorm = norms(x)
    half = means(blocks, K // 2)
    other = moved(half, "word", words, 1)
    near = nearest(half, x)
    cent, near = nearest(other, x, half, near, xnorm, owned=K // words)
    return cent, near.reshape(rows)


def summed(words, descriptors, word_ids):
    rows, depth = descriptors.shape
    keep, send, x = window_sums(word_ids.reshape(rows // 128, 128), descriptors)
    index = lax.axis_index("word")
    even = index % 2 == 0
    near_half = jnp.where(even, keep, send)
    far_half = jnp.where(even, send, keep)
    target = lax.broadcasted_iota(jnp.int32, (K // 2, HALF), 0)
    totals, counts = [], []
    for part in (near_half, far_half):
        aux = part[HALF, :SPREAD] + part[HALF, SPREAD:]
        hit = target == aux[None, :HALF].astype(jnp.int32)
        counts.append(jnp.sum(jnp.where(hit, aux[None, HALF:], 0.0), axis=1))
        totals.append(jnp.dot(hit.astype(F32), part[:HALF], precision=lax.Precision.HIGHEST))
    total, count = lax.psum((jnp.concatenate(totals), jnp.concatenate(counts)), BOTH)
    cent = (total / count[:, None]).astype(BF16)
    near = nearest(cent[: K // 2], x)
    unused, near = nearest(cent[K // 2 :], x, cent[: K // 2], near, norms(x), owned=SPREAD)
    cent = cent.reshape(2, K // SPREAD, HALF, depth).swapaxes(0, 1).reshape(K, depth)
    owned = K // words
    return lax.dynamic_slice_in_dim(cent, index * owned, owned, 0), near.reshape(rows)


def solution(mesh):
    groups, words = mesh.shape["grp"], mesh.shape["word"]
    small = groups * words * SPREAD <= 2 * K and K // words >= SPREAD
    return jax.shard_map(
        functools.partial(gathered, groups, words) if small else functools.partial(summed, words),
        mesh=mesh,
        in_specs=(P(BOTH, None), P(BOTH)),
        out_specs=(P("word", None), P(BOTH)),
        check_vma=False,
    )
```

```python
import functools

import jax
import jax.numpy as jnp
from jax import lax
from jax.experimental import pallas as pl
from jax.experimental.pallas import tpu as pltpu
from jax.sharding import PartitionSpec as P


K = 1024
SPREAD = 64
HALF = SPREAD // 2
AUX = 16
BOTH = ("grp", "word")
F32 = jnp.float32
I16 = jnp.int16
I32 = jnp.int32
TOP = 32767.0
BF16 = jnp.bfloat16
NT = (((1,), (1,)), ((), ()))
VMEM = pl.BlockSpec(memory_space=pltpu.VMEM)
HBM = pl.BlockSpec(memory_space=pltpu.HBM)
SMALL = pltpu.CompilerParams(vmem_limit_bytes=16 << 20)


def split3(v):
    hi = v.astype(BF16)
    rest = v - hi.astype(F32)
    mid = rest.astype(BF16)
    low = (rest - mid.astype(F32)).astype(BF16)
    return hi, mid, low


def half_of(groups, words):
    group, word = lax.axis_index("grp"), lax.axis_index("word")
    return (word + word // (words // 2) + group // (groups // 2)) % 2


def sums_kernel(ids_hbm, x_hbm, keep_ref, send_ref, x_ref, ids_ref, sem):
    half = half_of(lax.axis_size("grp"), lax.axis_size("word"))
    load_ids = pltpu.make_async_copy(ids_hbm, ids_ref, sem.at[0])
    load_ids.start()
    load = pltpu.make_async_copy(x_hbm, x_ref, sem.at[1])
    load.start()
    load_ids.wait()
    slot = lax.broadcasted_iota(I32, (SPREAD, 128), 0)
    ids = ids_ref[...]
    at = jnp.bitwise_and(ids, SPREAD - 1)
    total = jnp.zeros((SPREAD, 128), F32)
    pieces = []
    for r in range(ids.shape[0]):
        hit = jnp.where(slot == at[r : r + 1, :], 1.0, 0.0)
        total = total + hit
        pieces.append(hit.astype(BF16))
    first = ids[0:1, 0:1]
    rel = jnp.bitwise_and(ids - first + K // 2, K - 1)
    low = jnp.min(jnp.min(rel, axis=0, keepdims=True), axis=1, keepdims=True)
    start = jnp.bitwise_and(first + low - K // 2, K - 1)
    lane = lax.broadcasted_iota(I32, (AUX, 128), 1)
    line = lax.broadcasted_iota(I32, (AUX, 128), 0)
    own = jnp.bitwise_and(lane, SPREAD - 1)
    word = jnp.bitwise_and(start + jnp.bitwise_and(own - start, SPREAD - 1), K - 1)
    place = ((word // SPREAD) * HALF + jnp.bitwise_and(word, HALF - 1)).astype(F32)
    count = jnp.broadcast_to(jnp.sum(total, axis=1, keepdims=True), (SPREAD, 128))
    load.wait()
    sums = jnp.dot(jnp.concatenate(pieces, axis=1), x_ref[...], preferred_element_type=F32)
    largest = jnp.maximum(jnp.max(jnp.abs(sums), axis=1, keepdims=True), 2.0**-110)
    power = jnp.broadcast_to(jnp.floor(jnp.log2(largest)) - 14.0, (SPREAD, 128))
    rows = jnp.concatenate([count, power], axis=0).T
    stretch = rows[0:AUX, :]
    aux0 = jnp.where(line == 0, jnp.where(lane < HALF, place, pltpu.roll(stretch, HALF, 1)), pltpu.roll(stretch, SPREAD, 1))
    aux1 = jnp.where(line == 0, jnp.where(lane < HALF, pltpu.roll(place, 96, 1), stretch), pltpu.roll(stretch, HALF, 1))
    inside = jnp.logical_and(lane < SPREAD, line < 2)
    aux0 = jnp.where(inside, aux0, 0.0)
    aux1 = jnp.where(inside, aux1, 0.0)
    shift = jnp.exp2(-power).astype(BF16).astype(F32)
    code = jnp.clip(jnp.round(sums * shift), -TOP, TOP)
    keep = jnp.where(half == 0, code[0:HALF], code[HALF:SPREAD])
    send = jnp.where(half == 0, code[HALF:SPREAD], code[0:HALF])
    keep_ref[0:HALF, :] = keep.astype(I32).astype(I16)
    send_ref[0:HALF, :] = send.astype(I32).astype(I16)
    keep_ref[HALF : HALF + AUX, :] = jnp.where(half == 0, aux0, aux1).astype(I32).astype(I16)
    send_ref[HALF : HALF + AUX, :] = pltpu.roll(jnp.where(half == 0, aux1, aux0), SPREAD, 1).astype(I32).astype(I16)


def window_sums(ids, x):
    rows, depth = x.shape
    out = jax.ShapeDtypeStruct((HALF + AUX, depth), I16)
    return pl.pallas_call(
        sums_kernel,
        in_specs=[HBM, HBM],
        out_specs=(VMEM, VMEM, VMEM),
        out_shape=(out, out, jax.ShapeDtypeStruct(x.shape, x.dtype)),
        scratch_shapes=[pltpu.VMEM((rows // 128, 128), I32), pltpu.SemaphoreType.DMA((2,))],
        compiler_params=SMALL,
        name="window_sums",
    )(pltpu.with_memory_space_constraint(ids, pltpu.HBM), pltpu.with_memory_space_constraint(x, pltpu.HBM))


def norms_kernel(x_ref, out_ref):
    n = x_ref.shape[0]
    xf = x_ref[...].astype(F32)
    sq = xf * xf
    hi = sq.astype(BF16)
    low = (sq - hi.astype(F32)).astype(BF16)
    both = jnp.concatenate([hi, low], axis=1)
    ones = jnp.ones((8, both.shape[1]), BF16)
    row = lax.dot_general(ones, both, NT, preferred_element_type=F32)
    for r in range(n // 128):
        out_ref[r : r + 1, :] = row[0:1, r * 128 : (r + 1) * 128]


def norms(x):
    rows, depth = x.shape
    chunk = min(2048, rows)
    return pl.pallas_call(
        norms_kernel,
        grid=(rows // chunk,),
        in_specs=[pl.BlockSpec((chunk, depth), lambda i: (i, 0))],
        out_specs=pl.BlockSpec((chunk // 128, 128), lambda i: (i, 0)),
        out_shape=jax.ShapeDtypeStruct((rows // 128, 128), F32),
        cost_estimate=pl.CostEstimate(flops=2 * rows * depth, bytes_accessed=2 * rows * depth, transcendentals=0),
        compiler_params=SMALL,
        name="norms",
    )(x)


def means_kernel(parts, *refs):
    ins, table_ref = refs[:parts], refs[parts]
    rows = ins[0].shape[0] - AUX
    half = table_ref.shape[0]
    depth = ins[0].shape[1]
    target = lax.broadcasted_iota(I32, (half, 128), 0).astype(F32)
    lane = lax.broadcasted_iota(I32, (1, 128), 1)
    pieces, values = [], []
    count = jnp.zeros((half, 128), F32)
    for ref in ins:
        aux = ref[rows : rows + AUX, :].astype(I32).astype(F32)
        for pair in range(rows // 128):
            a, ea, b, eb = [aux[4 * pair + i : 4 * pair + i + 1, :] for i in range(4)]
            a32, b32 = pltpu.roll(a, 96, 1), pltpu.roll(b, 32, 1)
            place_a = jnp.where(lane < 32, a, a32)
            count_a = jnp.where(lane < 32, a32, pltpu.roll(a, 64, 1))
            power_a = jnp.where(lane < 32, ea, pltpu.roll(ea, 96, 1))
            place_b = jnp.where(lane < 96, pltpu.roll(b, 64, 1), b32)
            count_b = jnp.where(lane < 96, b32, b)
            power_b = jnp.where(lane < 96, pltpu.roll(eb, 64, 1), pltpu.roll(eb, 32, 1))
            place = jnp.where(lane < 64, place_a, place_b)
            amount = jnp.where(lane < 64, count_a, count_b)
            scale = jnp.exp2(jnp.where(lane < 64, power_a, power_b))
            hit = target == place
            count = count + jnp.where(hit, amount, 0.0)
            pieces.append(jnp.where(hit, scale, 0.0).astype(BF16))
            code = ref[128 * pair : 128 * pair + 128, :].astype(I32)
            high = jnp.bitwise_and(code + 128, -256)
            values.append(jnp.concatenate([high.astype(F32).astype(BF16), (code - high).astype(F32).astype(BF16)], axis=1))
    onehot = jnp.concatenate(pieces, axis=1)
    wide = jnp.dot(onehot, jnp.concatenate(values, axis=0), preferred_element_type=F32)
    sums = wide[:, 0:depth] + wide[:, depth : 2 * depth]
    cent = (sums / jnp.sum(count, axis=1, keepdims=True)).astype(BF16)
    write_table(cent, table_ref)


def write_table(cent, table_ref):
    words, depth = cent.shape
    cf = cent.astype(F32)
    norm = jnp.broadcast_to(-0.5 * jnp.sum(cf * cf, axis=1, keepdims=True), (words, depth))
    lane = lax.broadcasted_iota(I32, (words, depth), 1)
    hi, mid, low = [p.astype(F32) for p in split3(norm)]
    extra = jnp.where(lane == 0, hi, jnp.where(lane == 1, mid, jnp.where(lane == 2, low, 0.0)))
    table_ref[:, 0:depth] = cent
    table_ref[:, depth : 2 * depth] = extra.astype(BF16)


def table_kernel(cent_ref, table_ref):
    write_table(cent_ref[...], table_ref)


def tables(cent):
    words, depth = cent.shape
    return pl.pallas_call(
        table_kernel,
        in_specs=[VMEM],
        out_specs=VMEM,
        out_shape=jax.ShapeDtypeStruct((words, 2 * depth), BF16),
        compiler_params=SMALL,
        name="tables",
    )(cent)


def means(parts, half):
    depth = parts[0].shape[1]
    return pl.pallas_call(
        functools.partial(means_kernel, len(parts)),
        in_specs=[VMEM] * len(parts),
        out_specs=VMEM,
        compiler_params=SMALL,
        out_shape=jax.ShapeDtypeStruct((half, 2 * depth), BF16),
        name="means",
    )(*parts)


def own_words(mine_ref, other_ref, own_ref):
    index = lax.axis_index("word")
    even = half_of(lax.axis_size("grp"), lax.axis_size("word")) == 0
    blocks = own_ref.shape[0] // SPREAD
    for b in range(blocks):
        at = (index * blocks + b) % (mine_ref.shape[0] // HALF)
        rows = pl.ds(pl.multiple_of(at * HALF, HALF), HALF)
        mine, other = mine_ref[rows, 0 : own_ref.shape[1]], other_ref[rows, 0 : own_ref.shape[1]]
        own_ref[b * SPREAD : b * SPREAD + HALF, :] = jnp.where(even, mine, other)
        own_ref[b * SPREAD + HALF : (b + 1) * SPREAD, :] = jnp.where(even, other, mine)


def largest(table_ref, x_ref, out_ref, begin, end):
    words = table_ref.shape[0]
    depth = x_ref.shape[1]
    cols = 256
    ones = jnp.ones((cols, depth), BF16)
    for t in range(begin // cols, end // cols):
        full = jnp.concatenate([x_ref[t * cols : (t + 1) * cols, :], ones], axis=1)
        d = lax.dot_general(table_ref[...], full, NT, preferred_element_type=F32)
        row = jnp.max(jnp.max(d.reshape(words // 8, 8, cols), axis=0), axis=0, keepdims=True)
        for r in range(cols // 128):
            at = t * (cols // 128) + r
            out_ref[at : at + 1, :] = row[0:1, r * 128 : (r + 1) * 128]


def first_kernel(table_ref, x_ref, out_ref):
    largest(table_ref, x_ref, out_ref, 0, x_ref.shape[0])


def last_kernel(table_ref, x_ref, mine_ref, near_ref, norm_ref, own_hbm, out_hbm, own_ref, out_ref, sem):
    n, depth = x_ref.shape
    own_words(mine_ref, table_ref, own_ref)
    copies = [pltpu.make_async_copy(own_ref, own_hbm, sem.at[0])]
    copies[0].start()
    bounds = [0, n * 3 // 4, n]
    for i in range(2):
        begin, end = bounds[i], bounds[i + 1]
        largest(table_ref, x_ref, out_ref, begin, end)
        part = slice(begin // 128, end // 128)
        best = jnp.maximum(out_ref[part, :], near_ref[part, :])
        out_ref[part, :] = (norm_ref[part, :] - 2.0 * best) * (1.0 / depth)
        copies.append(pltpu.make_async_copy(out_ref.at[part, :], out_hbm.at[part, :], sem.at[i + 1]))
        copies[-1].start()
    for copy in copies:
        copy.wait()


def nearest_first(table, x):
    rows, depth = x.shape
    words = table.shape[0]
    return pl.pallas_call(
        first_kernel,
        in_specs=[VMEM, VMEM],
        out_specs=VMEM,
        out_shape=jax.ShapeDtypeStruct((rows // 128, 128), F32),
        cost_estimate=pl.CostEstimate(flops=4 * rows * depth * words, bytes_accessed=2 * rows * depth, transcendentals=0),
        compiler_params=SMALL,
        name="nearest_first",
    )(table, x)


def nearest_last(table, x, mine, near, norm, owned):
    rows, depth = x.shape
    words = table.shape[0]
    out, own = (rows // 128, 128), (owned, depth)
    return pl.pallas_call(
        last_kernel,
        in_specs=[VMEM] * 5,
        out_specs=(HBM, HBM),
        out_shape=(jax.ShapeDtypeStruct(own, BF16), jax.ShapeDtypeStruct(out, F32)),
        scratch_shapes=[pltpu.VMEM(own, BF16), pltpu.VMEM(out, F32), pltpu.SemaphoreType.DMA((3,))],
        cost_estimate=pl.CostEstimate(flops=4 * rows * depth * words, bytes_accessed=2 * rows * depth, transcendentals=0),
        compiler_params=SMALL,
        name="nearest_last",
    )(table, x, mine, near, norm)


def moved(a, groups, words, group=0, chip=0, core=0):
    core ^= group // (groups // 2) ^ chip // (words // 4)
    pairs = [(g * words + w, (g ^ group) * words + (w ^ (2 * chip + core))) for g in range(groups) for w in range(words)]
    return lax.ppermute(a, BOTH, pairs)


def chip_order(words):
    chips = words // 2
    return list(range(chips // 2, chips)) + list(range(1, chips // 2))


def group_order(groups):
    return list(range(groups - 1, 0, -1))


def gathered(groups, words, descriptors, word_ids):
    rows, depth = descriptors.shape
    ids = word_ids.reshape(rows // 128, 128)
    keep, send, x = window_sums(ids, descriptors)
    got = moved(send, groups, words, core=1)
    mine = jnp.concatenate([keep[:HALF], got[:HALF], keep[HALF:] + got[HALF:]], axis=0)
    line = [mine] + [moved(mine, groups, words, chip=k) for k in chip_order(words)]
    aux = [a[SPREAD : SPREAD + 2] for a in line]
    aux.append(jnp.zeros((-2 * len(line) % AUX, depth), I16))
    block = jnp.concatenate([a[:SPREAD] for a in line] + aux, axis=0)
    blocks = [block] + [moved(block, groups, words, group=k) for k in group_order(groups)]
    xnorm = norms(x)
    half = means(blocks, K // 2)
    other = moved(half, groups, words, core=1)
    near = nearest_first(half, x)
    cent, near = nearest_last(other, x, half, near, xnorm, K // words)
    return cent, near.reshape(rows)


def summed(words, descriptors, word_ids):
    rows, depth = descriptors.shape
    keep, send, x = window_sums(word_ids.reshape(rows // 128, 128), descriptors)
    index = lax.axis_index("word")
    even = half_of(lax.axis_size("grp"), lax.axis_size("word")) == 0
    near_half = jnp.where(even, keep, send)
    far_half = jnp.where(even, send, keep)
    target = lax.broadcasted_iota(I32, (K // 2, HALF), 0)
    totals, counts = [], []
    for part in (near_half, far_half):
        aux = (part[HALF : HALF + 2, :SPREAD] + part[HALF : HALF + 2, SPREAD:]).astype(I32)
        hit = target == aux[0:1, :HALF]
        counts.append(jnp.sum(jnp.where(hit, aux[0:1, HALF:].astype(F32), 0.0), axis=1))
        scale = jnp.exp2(aux[1, :HALF].astype(F32)).astype(BF16).astype(F32)
        totals.append(jnp.dot(hit.astype(F32), part[:HALF].astype(F32) * scale[:, None], precision=lax.Precision.HIGHEST))
    total, count = lax.psum((jnp.concatenate(totals), jnp.concatenate(counts)), BOTH)
    cent = (total / count[:, None]).astype(BF16)
    table = tables(cent)
    near = nearest_first(table[: K // 2], x)
    _, near = nearest_last(table[K // 2 :], x, table[: K // 2], near, norms(x), SPREAD)
    cent = cent.reshape(2, K // SPREAD, HALF, depth).swapaxes(0, 1).reshape(K, depth)
    owned = K // words
    return lax.dynamic_slice_in_dim(cent, index * owned, owned, 0), near.reshape(rows)


def solution(mesh):
    groups, words = mesh.shape["grp"], mesh.shape["word"]
    small = groups * words * SPREAD <= 2 * K and K // words >= SPREAD
    specs = dict(mesh=mesh, in_specs=(P(BOTH, None), P(BOTH)), out_specs=(P("word", None), P(BOTH)), check_vma=False)
    if not small:
        return jax.shard_map(functools.partial(summed, words), **specs)

    def step(descriptors, word_ids):
        return gathered(groups, words, descriptors, word_ids)

    return jax.shard_map(step, **specs)
```

```python
import functools

import jax
import jax.numpy as jnp
from jax import lax
from jax.experimental import pallas as pl
from jax.experimental.pallas import tpu as pltpu
from jax.sharding import PartitionSpec as P


K = 1024
SPREAD = 64
HALF = SPREAD // 2
AUX = 16
BOTH = ("grp", "word")
F32 = jnp.float32
I16 = jnp.int16
I32 = jnp.int32
TOP = 32767.0
BF16 = jnp.bfloat16
NT = (((1,), (1,)), ((), ()))
VMEM = pl.BlockSpec(memory_space=pltpu.VMEM)
HBM = pl.BlockSpec(memory_space=pltpu.HBM)
SMALL = pltpu.CompilerParams(vmem_limit_bytes=16 << 20)


def split3(v):
    hi = v.astype(BF16)
    rest = v - hi.astype(F32)
    mid = rest.astype(BF16)
    low = (rest - mid.astype(F32)).astype(BF16)
    return hi, mid, low


def bits(number, size):
    return sum((number // (1 << b)) % 2 for b in range(size.bit_length()))


def half_of(groups, words):
    group, word = lax.axis_index("grp"), lax.axis_index("word")
    return (word + bits(word // 2, words) + bits(group, groups)) % 2


def sums_kernel(ids_hbm, x_hbm, keep_ref, send_ref, x_ref, ids_ref, sem):
    half = half_of(lax.axis_size("grp"), lax.axis_size("word"))
    load_ids = pltpu.make_async_copy(ids_hbm, ids_ref, sem.at[0])
    load_ids.start()
    load = pltpu.make_async_copy(x_hbm, x_ref, sem.at[1])
    load.start()
    load_ids.wait()
    slot = lax.broadcasted_iota(I32, (SPREAD, 128), 0)
    ids = ids_ref[...]
    at = jnp.bitwise_and(ids, SPREAD - 1)
    total = jnp.zeros((SPREAD, 128), F32)
    pieces = []
    for r in range(ids.shape[0]):
        hit = jnp.where(slot == at[r : r + 1, :], 1.0, 0.0)
        total = total + hit
        pieces.append(hit.astype(BF16))
    first = ids[0:1, 0:1]
    rel = jnp.bitwise_and(ids - first + K // 2, K - 1)
    low = jnp.min(jnp.min(rel, axis=0, keepdims=True), axis=1, keepdims=True)
    start = jnp.bitwise_and(first + low - K // 2, K - 1)
    lane = lax.broadcasted_iota(I32, (AUX, 128), 1)
    line = lax.broadcasted_iota(I32, (AUX, 128), 0)
    own = jnp.bitwise_and(lane, SPREAD - 1)
    word = jnp.bitwise_and(start + jnp.bitwise_and(own - start, SPREAD - 1), K - 1)
    place = ((word // SPREAD) * HALF + jnp.bitwise_and(word, HALF - 1)).astype(F32)
    count = jnp.broadcast_to(jnp.sum(total, axis=1, keepdims=True), (SPREAD, 128))
    load.wait()
    sums = jnp.dot(jnp.concatenate(pieces, axis=1), x_ref[...], preferred_element_type=F32)
    largest = jnp.maximum(jnp.max(jnp.abs(sums), axis=1, keepdims=True), 2.0**-110)
    power = jnp.broadcast_to(jnp.floor(jnp.log2(largest)) - 14.0, (SPREAD, 128))
    rows = jnp.concatenate([count, power], axis=0).T
    stretch = rows[0:AUX, :]
    aux0 = jnp.where(line == 0, jnp.where(lane < HALF, place, pltpu.roll(stretch, HALF, 1)), pltpu.roll(stretch, SPREAD, 1))
    aux1 = jnp.where(line == 0, jnp.where(lane < HALF, pltpu.roll(place, 96, 1), stretch), pltpu.roll(stretch, HALF, 1))
    inside = jnp.logical_and(lane < SPREAD, line < 2)
    aux0 = jnp.where(inside, aux0, 0.0)
    aux1 = jnp.where(inside, aux1, 0.0)
    shift = jnp.exp2(-power).astype(BF16).astype(F32)
    code = jnp.clip(jnp.round(sums * shift), -TOP, TOP)
    keep = jnp.where(half == 0, code[0:HALF], code[HALF:SPREAD])
    send = jnp.where(half == 0, code[HALF:SPREAD], code[0:HALF])
    keep_ref[0:HALF, :] = keep.astype(I32).astype(I16)
    send_ref[0:HALF, :] = send.astype(I32).astype(I16)
    keep_ref[HALF : HALF + AUX, :] = jnp.where(half == 0, aux0, aux1).astype(I32).astype(I16)
    send_ref[HALF : HALF + AUX, :] = pltpu.roll(jnp.where(half == 0, aux1, aux0), SPREAD, 1).astype(I32).astype(I16)


def window_sums(ids, x):
    rows, depth = x.shape
    out = jax.ShapeDtypeStruct((HALF + AUX, depth), I16)
    return pl.pallas_call(
        sums_kernel,
        in_specs=[HBM, HBM],
        out_specs=(VMEM, VMEM, VMEM),
        out_shape=(out, out, jax.ShapeDtypeStruct(x.shape, x.dtype)),
        scratch_shapes=[pltpu.VMEM((rows // 128, 128), I32), pltpu.SemaphoreType.DMA((2,))],
        compiler_params=SMALL,
        name="window_sums",
    )(pltpu.with_memory_space_constraint(ids, pltpu.HBM), pltpu.with_memory_space_constraint(x, pltpu.HBM))


def norms_kernel(x_ref, out_ref):
    n = x_ref.shape[0]
    xf = x_ref[...].astype(F32)
    sq = xf * xf
    hi = sq.astype(BF16)
    low = (sq - hi.astype(F32)).astype(BF16)
    both = jnp.concatenate([hi, low], axis=1)
    ones = jnp.ones((8, both.shape[1]), BF16)
    row = lax.dot_general(ones, both, NT, preferred_element_type=F32)
    for r in range(n // 128):
        out_ref[r : r + 1, :] = row[0:1, r * 128 : (r + 1) * 128]


def norms(x):
    rows, depth = x.shape
    chunk = min(2048, rows)
    return pl.pallas_call(
        norms_kernel,
        grid=(rows // chunk,),
        in_specs=[pl.BlockSpec((chunk, depth), lambda i: (i, 0))],
        out_specs=pl.BlockSpec((chunk // 128, 128), lambda i: (i, 0)),
        out_shape=jax.ShapeDtypeStruct((rows // 128, 128), F32),
        cost_estimate=pl.CostEstimate(flops=2 * rows * depth, bytes_accessed=2 * rows * depth, transcendentals=0),
        compiler_params=SMALL,
        name="norms",
    )(x)


def means_kernel(parts, *refs):
    ins, table_ref = refs[:parts], refs[parts]
    rows = ins[0].shape[0] - AUX
    half = table_ref.shape[0]
    depth = ins[0].shape[1]
    target = lax.broadcasted_iota(I32, (half, 128), 0).astype(F32)
    lane = lax.broadcasted_iota(I32, (1, 128), 1)
    pieces, values = [], []
    count = jnp.zeros((half, 128), F32)
    for ref in ins:
        aux = ref[rows : rows + AUX, :].astype(I32).astype(F32)
        for pair in range(rows // 128):
            a, ea, b, eb = [aux[4 * pair + i : 4 * pair + i + 1, :] for i in range(4)]
            a32, b32 = pltpu.roll(a, 96, 1), pltpu.roll(b, 32, 1)
            place_a = jnp.where(lane < 32, a, a32)
            count_a = jnp.where(lane < 32, a32, pltpu.roll(a, 64, 1))
            power_a = jnp.where(lane < 32, ea, pltpu.roll(ea, 96, 1))
            place_b = jnp.where(lane < 96, pltpu.roll(b, 64, 1), b32)
            count_b = jnp.where(lane < 96, b32, b)
            power_b = jnp.where(lane < 96, pltpu.roll(eb, 64, 1), pltpu.roll(eb, 32, 1))
            place = jnp.where(lane < 64, place_a, place_b)
            amount = jnp.where(lane < 64, count_a, count_b)
            scale = jnp.exp2(jnp.where(lane < 64, power_a, power_b))
            hit = target == place
            count = count + jnp.where(hit, amount, 0.0)
            pieces.append(jnp.where(hit, scale, 0.0).astype(BF16))
            code = ref[128 * pair : 128 * pair + 128, :].astype(I32)
            high = jnp.bitwise_and(code + 128, -256)
            values.append(jnp.concatenate([high.astype(F32).astype(BF16), (code - high).astype(F32).astype(BF16)], axis=1))
    onehot = jnp.concatenate(pieces, axis=1)
    wide = jnp.dot(onehot, jnp.concatenate(values, axis=0), preferred_element_type=F32)
    sums = wide[:, 0:depth] + wide[:, depth : 2 * depth]
    cent = (sums / jnp.sum(count, axis=1, keepdims=True)).astype(BF16)
    write_table(cent, table_ref)


def write_table(cent, table_ref):
    words, depth = cent.shape
    cf = cent.astype(F32)
    norm = jnp.broadcast_to(-0.5 * jnp.sum(cf * cf, axis=1, keepdims=True), (words, depth))
    lane = lax.broadcasted_iota(I32, (words, depth), 1)
    hi, mid, low = [p.astype(F32) for p in split3(norm)]
    extra = jnp.where(lane == 0, hi, jnp.where(lane == 1, mid, jnp.where(lane == 2, low, 0.0)))
    table_ref[:, 0:depth] = cent
    table_ref[:, depth : 2 * depth] = extra.astype(BF16)


def table_kernel(cent_ref, table_ref):
    write_table(cent_ref[...], table_ref)


def tables(cent):
    words, depth = cent.shape
    return pl.pallas_call(
        table_kernel,
        in_specs=[VMEM],
        out_specs=VMEM,
        out_shape=jax.ShapeDtypeStruct((words, 2 * depth), BF16),
        compiler_params=SMALL,
        name="tables",
    )(cent)


def means(parts, half):
    depth = parts[0].shape[1]
    return pl.pallas_call(
        functools.partial(means_kernel, len(parts)),
        in_specs=[VMEM] * len(parts),
        out_specs=VMEM,
        compiler_params=SMALL,
        out_shape=jax.ShapeDtypeStruct((half, 2 * depth), BF16),
        name="means",
    )(*parts)


def own_words(mine_ref, other_ref, own_ref):
    index = lax.axis_index("word")
    even = half_of(lax.axis_size("grp"), lax.axis_size("word")) == 0
    blocks = own_ref.shape[0] // SPREAD
    for b in range(blocks):
        at = (index * blocks + b) % (mine_ref.shape[0] // HALF)
        rows = pl.ds(pl.multiple_of(at * HALF, HALF), HALF)
        mine, other = mine_ref[rows, 0 : own_ref.shape[1]], other_ref[rows, 0 : own_ref.shape[1]]
        own_ref[b * SPREAD : b * SPREAD + HALF, :] = jnp.where(even, mine, other)
        own_ref[b * SPREAD + HALF : (b + 1) * SPREAD, :] = jnp.where(even, other, mine)


def largest(table_ref, x_ref, out_ref, begin, end):
    words = table_ref.shape[0]
    depth = x_ref.shape[1]
    cols = 256
    ones = jnp.ones((cols, depth), BF16)
    for t in range(begin // cols, end // cols):
        full = jnp.concatenate([x_ref[t * cols : (t + 1) * cols, :], ones], axis=1)
        d = lax.dot_general(table_ref[...], full, NT, preferred_element_type=F32)
        row = jnp.max(jnp.max(d.reshape(words // 8, 8, cols), axis=0), axis=0, keepdims=True)
        for r in range(cols // 128):
            at = t * (cols // 128) + r
            out_ref[at : at + 1, :] = row[0:1, r * 128 : (r + 1) * 128]


def first_kernel(table_ref, x_ref, out_ref):
    largest(table_ref, x_ref, out_ref, 0, x_ref.shape[0])


def last_kernel(table_ref, x_ref, mine_ref, near_ref, norm_ref, own_hbm, out_hbm, own_ref, out_ref, sem):
    n, depth = x_ref.shape
    own_words(mine_ref, table_ref, own_ref)
    copies = [pltpu.make_async_copy(own_ref, own_hbm, sem.at[0])]
    copies[0].start()
    bounds = [0, n * 3 // 4, n]
    for i in range(2):
        begin, end = bounds[i], bounds[i + 1]
        largest(table_ref, x_ref, out_ref, begin, end)
        part = slice(begin // 128, end // 128)
        best = jnp.maximum(out_ref[part, :], near_ref[part, :])
        out_ref[part, :] = (norm_ref[part, :] - 2.0 * best) * (1.0 / depth)
        copies.append(pltpu.make_async_copy(out_ref.at[part, :], out_hbm.at[part, :], sem.at[i + 1]))
        copies[-1].start()
    for copy in copies:
        copy.wait()


def nearest_first(table, x):
    rows, depth = x.shape
    words = table.shape[0]
    return pl.pallas_call(
        first_kernel,
        in_specs=[VMEM, VMEM],
        out_specs=VMEM,
        out_shape=jax.ShapeDtypeStruct((rows // 128, 128), F32),
        cost_estimate=pl.CostEstimate(flops=4 * rows * depth * words, bytes_accessed=2 * rows * depth, transcendentals=0),
        compiler_params=SMALL,
        name="nearest_first",
    )(table, x)


def nearest_last(table, x, mine, near, norm, owned):
    rows, depth = x.shape
    words = table.shape[0]
    out, own = (rows // 128, 128), (owned, depth)
    return pl.pallas_call(
        last_kernel,
        in_specs=[VMEM] * 5,
        out_specs=(HBM, HBM),
        out_shape=(jax.ShapeDtypeStruct(own, BF16), jax.ShapeDtypeStruct(out, F32)),
        scratch_shapes=[pltpu.VMEM(own, BF16), pltpu.VMEM(out, F32), pltpu.SemaphoreType.DMA((3,))],
        cost_estimate=pl.CostEstimate(flops=4 * rows * depth * words, bytes_accessed=2 * rows * depth, transcendentals=0),
        compiler_params=SMALL,
        name="nearest_last",
    )(table, x, mine, near, norm)


def moved(a, groups, words, group=0, chip=0, core=0):
    core ^= (bits(group, groups) + bits(chip, words)) % 2
    pairs = [(g * words + w, (g ^ group) * words + (w ^ (2 * chip + core))) for g in range(groups) for w in range(words)]
    return lax.ppermute(a, BOTH, pairs)


def group_order(groups):
    return list(range(groups - 1, 0, -1))


def gathered(groups, words, descriptors, word_ids):
    rows, depth = descriptors.shape
    ids = word_ids.reshape(rows // 128, 128)
    keep, send, x = window_sums(ids, descriptors)
    got = moved(send, groups, words, core=1)
    mine = jnp.concatenate([keep[:HALF], got[:HALF], keep[HALF:] + got[HALF:]], axis=0)
    lines = mine[None]
    chip = words // 4
    while chip:
        met = moved(lines.reshape(-1, depth), groups, words, chip=chip)
        lines = jnp.concatenate([lines, met.reshape(lines.shape)], axis=0)
        chip //= 2
    line = list(lines)
    aux = [a[SPREAD : SPREAD + 2] for a in line]
    aux.append(jnp.zeros((-2 * len(line) % AUX, depth), I16))
    block = jnp.concatenate([a[:SPREAD] for a in line] + aux, axis=0)
    blocks = [block] + [moved(block, groups, words, group=k) for k in group_order(groups)]
    xnorm = norms(x)
    half = means(blocks, K // 2)
    other = moved(half, groups, words, core=1)
    near = nearest_first(half, x)
    cent, near = nearest_last(other, x, half, near, xnorm, K // words)
    return cent, near.reshape(rows)


def summed(words, descriptors, word_ids):
    rows, depth = descriptors.shape
    keep, send, x = window_sums(word_ids.reshape(rows // 128, 128), descriptors)
    index = lax.axis_index("word")
    even = half_of(lax.axis_size("grp"), lax.axis_size("word")) == 0
    near_half = jnp.where(even, keep, send)
    far_half = jnp.where(even, send, keep)
    target = lax.broadcasted_iota(I32, (K // 2, HALF), 0)
    totals, counts = [], []
    for part in (near_half, far_half):
        aux = (part[HALF : HALF + 2, :SPREAD] + part[HALF : HALF + 2, SPREAD:]).astype(I32)
        hit = target == aux[0:1, :HALF]
        counts.append(jnp.sum(jnp.where(hit, aux[0:1, HALF:].astype(F32), 0.0), axis=1))
        scale = jnp.exp2(aux[1, :HALF].astype(F32)).astype(BF16).astype(F32)
        totals.append(jnp.dot(hit.astype(F32), part[:HALF].astype(F32) * scale[:, None], precision=lax.Precision.HIGHEST))
    total, count = lax.psum((jnp.concatenate(totals), jnp.concatenate(counts)), BOTH)
    cent = (total / count[:, None]).astype(BF16)
    table = tables(cent)
    near = nearest_first(table[: K // 2], x)
    _, near = nearest_last(table[K // 2 :], x, table[: K // 2], near, norms(x), SPREAD)
    cent = cent.reshape(2, K // SPREAD, HALF, depth).swapaxes(0, 1).reshape(K, depth)
    owned = K // words
    return lax.dynamic_slice_in_dim(cent, index * owned, owned, 0), near.reshape(rows)


def solution(mesh):
    groups, words = mesh.shape["grp"], mesh.shape["word"]
    small = groups * words * SPREAD <= 2 * K and K // words >= SPREAD
    specs = dict(mesh=mesh, in_specs=(P(BOTH, None), P(BOTH)), out_specs=(P("word", None), P(BOTH)), check_vma=False)
    if not small:
        return jax.shard_map(functools.partial(summed, words), **specs)

    def step(descriptors, word_ids):
        return gathered(groups, words, descriptors, word_ids)

    return jax.shard_map(step, **specs)
```

```python
import functools

import jax
import jax.numpy as jnp
from jax import lax
from jax.experimental import pallas as pl
from jax.experimental.pallas import tpu as pltpu
from jax.sharding import PartitionSpec as P


K = 1024
SPREAD = 64
HALF = SPREAD // 2
AUX = 16
BOTH = ("grp", "word")
F32 = jnp.float32
I16 = jnp.int16
I32 = jnp.int32
TOP = 32767.0
BF16 = jnp.bfloat16
NT = (((1,), (1,)), ((), ()))
VMEM = pl.BlockSpec(memory_space=pltpu.VMEM)
HBM = pl.BlockSpec(memory_space=pltpu.HBM)
SMALL = pltpu.CompilerParams(vmem_limit_bytes=16 << 20)


def split3(v):
    hi = v.astype(BF16)
    rest = v - hi.astype(F32)
    mid = rest.astype(BF16)
    low = (rest - mid.astype(F32)).astype(BF16)
    return hi, mid, low


def bits(number, size):
    return sum((number // (1 << b)) % 2 for b in range(size.bit_length()))


def half_of(groups, words):
    group, word = lax.axis_index("grp"), lax.axis_index("word")
    return (word + bits(word // 2, words) + bits(group, groups)) % 2


def sums_kernel(ids_hbm, x_hbm, keep_ref, send_ref, x_ref, ids_ref, sem):
    half = half_of(lax.axis_size("grp"), lax.axis_size("word"))
    load_ids = pltpu.make_async_copy(ids_hbm, ids_ref, sem.at[0])
    load_ids.start()
    cuts = (slice(0, x_ref.shape[0] // 2), slice(x_ref.shape[0] // 2, x_ref.shape[0]))
    loads = [pltpu.make_async_copy(x_hbm.at[c, :], x_ref.at[c, :], sem.at[1 + i]) for i, c in enumerate(cuts)]
    for load in loads:
        load.start()
    load_ids.wait()
    slot = lax.broadcasted_iota(I32, (SPREAD, 128), 0)
    ids = ids_ref[...]
    at = jnp.bitwise_and(ids, SPREAD - 1)
    total = jnp.zeros((SPREAD, 128), F32)
    pieces = []
    for r in range(ids.shape[0]):
        hit = jnp.where(slot == at[r : r + 1, :], 1.0, 0.0)
        total = total + hit
        pieces.append(hit.astype(BF16))
    first = ids[0:1, 0:1]
    rel = jnp.bitwise_and(ids - first + K // 2, K - 1)
    low = jnp.min(jnp.min(rel, axis=0, keepdims=True), axis=1, keepdims=True)
    start = jnp.bitwise_and(first + low - K // 2, K - 1)
    lane = lax.broadcasted_iota(I32, (AUX, 128), 1)
    line = lax.broadcasted_iota(I32, (AUX, 128), 0)
    own = jnp.bitwise_and(lane, SPREAD - 1)
    word = jnp.bitwise_and(start + jnp.bitwise_and(own - start, SPREAD - 1), K - 1)
    place = ((word // SPREAD) * HALF + jnp.bitwise_and(word, HALF - 1)).astype(F32)
    count = jnp.broadcast_to(jnp.sum(total, axis=1, keepdims=True), (SPREAD, 128))
    onehot = jnp.concatenate(pieces, axis=1)
    sums = jnp.zeros((SPREAD, x_ref.shape[1]), F32)
    for load, c in zip(loads, cuts):
        load.wait()
        sums = sums + jnp.dot(onehot[:, c], x_ref[c, :], preferred_element_type=F32)
    largest = jnp.maximum(jnp.max(jnp.abs(sums), axis=1, keepdims=True), 2.0**-110)
    power = jnp.broadcast_to(jnp.floor(jnp.log2(largest)) - 14.0, (SPREAD, 128))
    rows = jnp.concatenate([count, power], axis=0).T
    stretch = rows[0:AUX, :]
    aux0 = jnp.where(line == 0, jnp.where(lane < HALF, place, pltpu.roll(stretch, HALF, 1)), pltpu.roll(stretch, SPREAD, 1))
    aux1 = jnp.where(line == 0, jnp.where(lane < HALF, pltpu.roll(place, 96, 1), stretch), pltpu.roll(stretch, HALF, 1))
    inside = jnp.logical_and(lane < SPREAD, line < 2)
    aux0 = jnp.where(inside, aux0, 0.0)
    aux1 = jnp.where(inside, aux1, 0.0)
    shift = jnp.exp2(-power).astype(BF16).astype(F32)
    code = jnp.clip(jnp.round(sums * shift), -TOP, TOP)
    keep = jnp.where(half == 0, code[0:HALF], code[HALF:SPREAD])
    send = jnp.where(half == 0, code[HALF:SPREAD], code[0:HALF])
    keep_ref[0:HALF, :] = keep.astype(I32).astype(I16)
    send_ref[0:HALF, :] = send.astype(I32).astype(I16)
    keep_ref[HALF : HALF + AUX, :] = jnp.where(half == 0, aux0, aux1).astype(I32).astype(I16)
    send_ref[HALF : HALF + AUX, :] = pltpu.roll(jnp.where(half == 0, aux1, aux0), SPREAD, 1).astype(I32).astype(I16)


def window_sums(ids, x):
    rows, depth = x.shape
    out = jax.ShapeDtypeStruct((HALF + AUX, depth), I16)
    return pl.pallas_call(
        sums_kernel,
        in_specs=[HBM, HBM],
        out_specs=(VMEM, VMEM, VMEM),
        out_shape=(out, out, jax.ShapeDtypeStruct(x.shape, x.dtype)),
        scratch_shapes=[pltpu.VMEM((rows // 128, 128), I32), pltpu.SemaphoreType.DMA((3,))],
        compiler_params=SMALL,
        name="window_sums",
    )(pltpu.with_memory_space_constraint(ids, pltpu.HBM), pltpu.with_memory_space_constraint(x, pltpu.HBM))


def norms_kernel(x_ref, out_ref):
    n = x_ref.shape[0]
    xf = x_ref[...].astype(F32)
    sq = xf * xf
    hi = sq.astype(BF16)
    low = (sq - hi.astype(F32)).astype(BF16)
    both = jnp.concatenate([hi, low], axis=1)
    ones = jnp.ones((8, both.shape[1]), BF16)
    row = lax.dot_general(ones, both, NT, preferred_element_type=F32)
    for r in range(n // 128):
        out_ref[r : r + 1, :] = row[0:1, r * 128 : (r + 1) * 128]


def norms(x):
    rows, depth = x.shape
    chunk = min(2048, rows)
    return pl.pallas_call(
        norms_kernel,
        grid=(rows // chunk,),
        in_specs=[pl.BlockSpec((chunk, depth), lambda i: (i, 0))],
        out_specs=pl.BlockSpec((chunk // 128, 128), lambda i: (i, 0)),
        out_shape=jax.ShapeDtypeStruct((rows // 128, 128), F32),
        cost_estimate=pl.CostEstimate(flops=2 * rows * depth, bytes_accessed=2 * rows * depth, transcendentals=0),
        compiler_params=SMALL,
        name="norms",
    )(x)


def means_kernel(parts, *refs):
    ins, table_ref = refs[:parts], refs[parts]
    rows = ins[0].shape[0] - AUX
    half = table_ref.shape[0]
    depth = ins[0].shape[1]
    target = lax.broadcasted_iota(I32, (half, 128), 0).astype(F32)
    lane = lax.broadcasted_iota(I32, (1, 128), 1)
    pieces, values = [], []
    count = jnp.zeros((half, 128), F32)
    for ref in ins:
        aux = ref[rows : rows + AUX, :].astype(I32).astype(F32)
        for pair in range(rows // 128):
            a, ea, b, eb = [aux[4 * pair + i : 4 * pair + i + 1, :] for i in range(4)]
            a32, b32 = pltpu.roll(a, 96, 1), pltpu.roll(b, 32, 1)
            place_a = jnp.where(lane < 32, a, a32)
            count_a = jnp.where(lane < 32, a32, pltpu.roll(a, 64, 1))
            power_a = jnp.where(lane < 32, ea, pltpu.roll(ea, 96, 1))
            place_b = jnp.where(lane < 96, pltpu.roll(b, 64, 1), b32)
            count_b = jnp.where(lane < 96, b32, b)
            power_b = jnp.where(lane < 96, pltpu.roll(eb, 64, 1), pltpu.roll(eb, 32, 1))
            place = jnp.where(lane < 64, place_a, place_b)
            amount = jnp.where(lane < 64, count_a, count_b)
            scale = jnp.exp2(jnp.where(lane < 64, power_a, power_b))
            hit = target == place
            count = count + jnp.where(hit, amount, 0.0)
            pieces.append(jnp.where(hit, scale, 0.0).astype(BF16))
            code = ref[128 * pair : 128 * pair + 128, :].astype(I32)
            high = jnp.bitwise_and(code + 128, -256)
            values.append(jnp.concatenate([high.astype(F32).astype(BF16), (code - high).astype(F32).astype(BF16)], axis=1))
    onehot = jnp.concatenate(pieces, axis=1)
    wide = jnp.dot(onehot, jnp.concatenate(values, axis=0), preferred_element_type=F32)
    sums = wide[:, 0:depth] + wide[:, depth : 2 * depth]
    cent = (sums / jnp.sum(count, axis=1, keepdims=True)).astype(BF16)
    write_table(cent, table_ref)


def write_table(cent, table_ref):
    words, depth = cent.shape
    cf = cent.astype(F32)
    norm = jnp.broadcast_to(-0.5 * jnp.sum(cf * cf, axis=1, keepdims=True), (words, depth))
    lane = lax.broadcasted_iota(I32, (words, depth), 1)
    hi, mid, low = [p.astype(F32) for p in split3(norm)]
    extra = jnp.where(lane == 0, hi, jnp.where(lane == 1, mid, jnp.where(lane == 2, low, 0.0)))
    table_ref[:, 0:depth] = cent
    table_ref[:, depth : 2 * depth] = extra.astype(BF16)


def table_kernel(cent_ref, table_ref):
    write_table(cent_ref[...], table_ref)


def tables(cent):
    words, depth = cent.shape
    return pl.pallas_call(
        table_kernel,
        in_specs=[VMEM],
        out_specs=VMEM,
        out_shape=jax.ShapeDtypeStruct((words, 2 * depth), BF16),
        compiler_params=SMALL,
        name="tables",
    )(cent)


def means(parts, half):
    depth = parts[0].shape[1]
    return pl.pallas_call(
        functools.partial(means_kernel, len(parts)),
        in_specs=[VMEM] * len(parts),
        out_specs=VMEM,
        compiler_params=SMALL,
        out_shape=jax.ShapeDtypeStruct((half, 2 * depth), BF16),
        name="means",
    )(*parts)


def own_words(mine_ref, other_ref, own_ref):
    index = lax.axis_index("word")
    even = half_of(lax.axis_size("grp"), lax.axis_size("word")) == 0
    blocks = own_ref.shape[0] // SPREAD
    for b in range(blocks):
        at = (index * blocks + b) % (mine_ref.shape[0] // HALF)
        rows = pl.ds(pl.multiple_of(at * HALF, HALF), HALF)
        mine, other = mine_ref[rows, 0 : own_ref.shape[1]], other_ref[rows, 0 : own_ref.shape[1]]
        own_ref[b * SPREAD : b * SPREAD + HALF, :] = jnp.where(even, mine, other)
        own_ref[b * SPREAD + HALF : (b + 1) * SPREAD, :] = jnp.where(even, other, mine)


def largest(table_ref, x_ref, out_ref, begin, end):
    words = table_ref.shape[0]
    depth = x_ref.shape[1]
    cols = 256
    ones = jnp.ones((cols, depth), BF16)
    for t in range(begin // cols, end // cols):
        full = jnp.concatenate([x_ref[t * cols : (t + 1) * cols, :], ones], axis=1)
        d = lax.dot_general(table_ref[...], full, NT, preferred_element_type=F32)
        row = jnp.max(jnp.max(d.reshape(words // 8, 8, cols), axis=0), axis=0, keepdims=True)
        for r in range(cols // 128):
            at = t * (cols // 128) + r
            out_ref[at : at + 1, :] = row[0:1, r * 128 : (r + 1) * 128]


def first_kernel(table_ref, x_ref, out_ref):
    largest(table_ref, x_ref, out_ref, 0, x_ref.shape[0])


def last_kernel(table_ref, x_ref, mine_ref, near_ref, norm_ref, own_hbm, out_hbm, own_ref, out_ref, sem):
    n, depth = x_ref.shape
    own_words(mine_ref, table_ref, own_ref)
    copies = [pltpu.make_async_copy(own_ref, own_hbm, sem.at[0])]
    copies[0].start()
    bounds = [0, n * 3 // 4, n]
    for i in range(2):
        begin, end = bounds[i], bounds[i + 1]
        largest(table_ref, x_ref, out_ref, begin, end)
        part = slice(begin // 128, end // 128)
        best = jnp.maximum(out_ref[part, :], near_ref[part, :])
        out_ref[part, :] = (norm_ref[part, :] - 2.0 * best) * (1.0 / depth)
        copies.append(pltpu.make_async_copy(out_ref.at[part, :], out_hbm.at[part, :], sem.at[i + 1]))
        copies[-1].start()
    for copy in copies:
        copy.wait()


def nearest_first(table, x):
    rows, depth = x.shape
    words = table.shape[0]
    return pl.pallas_call(
        first_kernel,
        in_specs=[VMEM, VMEM],
        out_specs=VMEM,
        out_shape=jax.ShapeDtypeStruct((rows // 128, 128), F32),
        cost_estimate=pl.CostEstimate(flops=4 * rows * depth * words, bytes_accessed=2 * rows * depth, transcendentals=0),
        compiler_params=SMALL,
        name="nearest_first",
    )(table, x)


def nearest_last(table, x, mine, near, norm, owned):
    rows, depth = x.shape
    words = table.shape[0]
    out, own = (rows // 128, 128), (owned, depth)
    return pl.pallas_call(
        last_kernel,
        in_specs=[VMEM] * 5,
        out_specs=(HBM, HBM),
        out_shape=(jax.ShapeDtypeStruct(own, BF16), jax.ShapeDtypeStruct(out, F32)),
        scratch_shapes=[pltpu.VMEM(own, BF16), pltpu.VMEM(out, F32), pltpu.SemaphoreType.DMA((3,))],
        cost_estimate=pl.CostEstimate(flops=4 * rows * depth * words, bytes_accessed=2 * rows * depth, transcendentals=0),
        compiler_params=SMALL,
        name="nearest_last",
    )(table, x, mine, near, norm)


def moved(a, groups, words, group=0, chip=0, core=0):
    core ^= (bits(group, groups) + bits(chip, words)) % 2
    pairs = [(g * words + w, (g ^ group) * words + (w ^ (2 * chip + core))) for g in range(groups) for w in range(words)]
    return lax.ppermute(a, BOTH, pairs)


def group_order(groups):
    return list(range(groups - 1, 0, -1))


def gathered(groups, words, descriptors, word_ids):
    rows, depth = descriptors.shape
    ids = word_ids.reshape(rows // 128, 128)
    keep, send, x = window_sums(ids, descriptors)
    got = moved(send, groups, words, core=1)
    mine = jnp.concatenate([keep[:HALF], got[:HALF], keep[HALF:] + got[HALF:]], axis=0)
    lines = mine[None]
    chip = words // 4
    while chip:
        met = moved(lines.reshape(-1, depth), groups, words, chip=chip)
        lines = jnp.concatenate([lines, met.reshape(lines.shape)], axis=0)
        chip //= 2
    line = list(lines)
    aux = [a[SPREAD : SPREAD + 2] for a in line]
    aux.append(jnp.zeros((-2 * len(line) % AUX, depth), I16))
    block = jnp.concatenate([a[:SPREAD] for a in line] + aux, axis=0)
    blocks = [block] + [moved(block, groups, words, group=k) for k in group_order(groups)]
    xnorm = norms(x)
    half = means(blocks, K // 2)
    other = moved(half, groups, words, core=1)
    near = nearest_first(half, x)
    cent, near = nearest_last(other, x, half, near, xnorm, K // words)
    return cent, near.reshape(rows)


def summed(words, descriptors, word_ids):
    rows, depth = descriptors.shape
    keep, send, x = window_sums(word_ids.reshape(rows // 128, 128), descriptors)
    index = lax.axis_index("word")
    even = half_of(lax.axis_size("grp"), lax.axis_size("word")) == 0
    near_half = jnp.where(even, keep, send)
    far_half = jnp.where(even, send, keep)
    target = lax.broadcasted_iota(I32, (K // 2, HALF), 0)
    totals, counts = [], []
    for part in (near_half, far_half):
        aux = (part[HALF : HALF + 2, :SPREAD] + part[HALF : HALF + 2, SPREAD:]).astype(I32)
        hit = target == aux[0:1, :HALF]
        counts.append(jnp.sum(jnp.where(hit, aux[0:1, HALF:].astype(F32), 0.0), axis=1))
        scale = jnp.exp2(aux[1, :HALF].astype(F32)).astype(BF16).astype(F32)
        totals.append(jnp.dot(hit.astype(F32), part[:HALF].astype(F32) * scale[:, None], precision=lax.Precision.HIGHEST))
    total, count = lax.psum((jnp.concatenate(totals), jnp.concatenate(counts)), BOTH)
    cent = (total / count[:, None]).astype(BF16)
    table = tables(cent)
    near = nearest_first(table[: K // 2], x)
    _, near = nearest_last(table[K // 2 :], x, table[: K // 2], near, norms(x), SPREAD)
    cent = cent.reshape(2, K // SPREAD, HALF, depth).swapaxes(0, 1).reshape(K, depth)
    owned = K // words
    return lax.dynamic_slice_in_dim(cent, index * owned, owned, 0), near.reshape(rows)


def solution(mesh):
    groups, words = mesh.shape["grp"], mesh.shape["word"]
    small = groups * words * SPREAD <= 2 * K and K // words >= SPREAD
    specs = dict(mesh=mesh, in_specs=(P(BOTH, None), P(BOTH)), out_specs=(P("word", None), P(BOTH)), check_vma=False)
    if not small:
        return jax.shard_map(functools.partial(summed, words), **specs)

    def step(descriptors, word_ids):
        return gathered(groups, words, descriptors, word_ids)

    return jax.shard_map(step, **specs)
```
